32 devices in a mesh: ctx: 16 (over z, y, x), head: 2 (over core).
Axes of the slice: x: 2, y: 2, z: 4, core: 2. Of those that a mesh axis runs over, the one named last changes fastest.
Arguments:
- queries: bfloat16 [8192, 4, 4, 128], P('ctx', 'head')
- keys: bfloat16 [8192, 4, 128], P('ctx')
- values: bfloat16 [8192, 4, 128], P('ctx'), may hold values from -6 to 6
- output_gradient: bfloat16 [8192, 4, 4, 128], P('ctx', 'head'), may hold values from -6 to 6
- selected: int32 [16, 2], replicated, may hold values from 0 to 14, as said below
Outputs:
- attn_out: bfloat16 [8192, 4, 4, 128], P('ctx', 'head')
- grad_q: bfloat16 [8192, 4, 4, 128], P('ctx', 'head')
- grad_k: bfloat16 [8192, 4, 128], P('ctx', 'head')
- grad_v: bfloat16 [8192, 4, 128], P('ctx', 'head')
The draws below stay inside these ranges and needn't reach their ends.
Inputs may be any that keep to these rules, and one draw needn't show every extreme that they name: selected[b, j] <= b for every block b; an entry equal to b selects no block; for b >= 2 the two entries of a row differ and both are below b.
All inputs are finite; a program needn't handle non-finite values.
Results may differ from the reference program's by a relative error of at most 0.011.
Values may be sent and summed in bfloat16 or wider, within the bound.
A program may use at most 128 MiB of HBM per device.

```python
import jax
import jax.numpy as jnp
from jax import lax

KEY_VALUE_HEADS = 4
QUERY_PER_KEY = 4
HEAD_DIMENSION = 128
BLK = 512
NB = 16
SEQUENCE_TOKENS = 8192


def draw_keys(key, part):
    return jnp.clip(jax.random.normal(jax.random.fold_in(key, 11), (SEQUENCE_TOKENS, KEY_VALUE_HEADS, HEAD_DIMENSION), jnp.float32), -6.0, 6.0).astype(jnp.bfloat16)


def draw_queries(key, part):
    return jnp.clip(jax.random.normal(jax.random.fold_in(key, 12), (SEQUENCE_TOKENS, QUERY_PER_KEY, KEY_VALUE_HEADS, HEAD_DIMENSION), jnp.float32), -6.0, 6.0).astype(jnp.bfloat16)


def draw_selected(key, part):
    index = jnp.arange(NB, dtype=jnp.int32)
    hottest = jax.random.randint(jax.random.fold_in(key, 1), (), 0, NB // 4)
    coin_flip = jax.random.randint(jax.random.fold_in(key, 2), (NB,), 0, 2)
    first_pick = jax.random.randint(jax.random.fold_in(key, 3), (NB,), 0, jnp.maximum(index, 1))
    first_pick = jnp.where((coin_flip == 1) & (index > hottest), hottest, first_pick)
    other_pick = jax.random.randint(jax.random.fold_in(key, 4), (NB,), 0, jnp.maximum(index - 1, 1))
    second_pick = other_pick + (other_pick >= first_pick).astype(jnp.int32)
    second_pick = jnp.where(index == 0, 0, second_pick)
    first_pick = jnp.where(index == NB - 1, hottest, first_pick)
    second_pick = jnp.where(index == NB - 1, NB - 2, second_pick)
    return jnp.stack([first_pick, second_pick], axis=1).astype(jnp.int32)


def steps_of(rng, dims, shards, low, high):
    def one(axis_at, parts):
        heights = jax.random.uniform(jax.random.fold_in(jax.random.fold_in(rng, 6), axis_at), (parts,), jnp.float32, low / len(shards), high / len(shards))
        return jnp.repeat(jnp.exp(heights), dims[axis_at] // parts).reshape((-1,) + (1,) * (len(dims) - axis_at - 1))

    factor_of = one(*shards[0])
    for cut in shards[1:]:
        factor_of = factor_of * one(*cut)
    return factor_of


def normal_values(own_key, dims, deviation, limit, cuts=(), kind=jnp.bfloat16):
    drawn = jax.random.normal(own_key, dims, jnp.float32) * deviation
    if len(cuts) > 0:
        drawn = steps_of(own_key, dims, cuts, -0.22, 0.18) * drawn
    return jnp.clip(drawn, min=-limit, max=limit).astype(kind)


def setup_inputs(seed: int = 0) -> dict:
    streams_of = jax.random.split(jax.random.key(seed), 6)
    return {
        "queries": draw_queries(jax.random.fold_in(streams_of[5], 71), 0),
        "keys": draw_keys(jax.random.fold_in(streams_of[5], 71), 0),
        "values": normal_values(streams_of[2], (SEQUENCE_TOKENS, KEY_VALUE_HEADS, HEAD_DIMENSION), 1.0, 6.0, ((0, 16),)),
        "output_gradient": normal_values(streams_of[3], (SEQUENCE_TOKENS, QUERY_PER_KEY, KEY_VALUE_HEADS, HEAD_DIMENSION), 1.0, 6.0, ((0, 16), (1, 2))),
        "selected": draw_selected(jax.random.fold_in(streams_of[5], 71), 0),
    }


def attend_block(block_q, block_k, block_v, block_g, visible, softmax_scale):
    query_f = block_q.astype(jnp.float32)
    key_f = block_k.astype(jnp.float32)
    value_f = block_v.astype(jnp.float32)
    grad_f = block_g.astype(jnp.float32)
    scores = jnp.einsum("qgnd,knd->gnqk", query_f, key_f) * softmax_scale
    scores = jnp.where(visible, scores, -jnp.inf)
    row_max = jnp.max(scores, axis=-1, keepdims=True)
    weights = jnp.exp(scores - row_max)
    probs = weights / jnp.sum(weights, axis=-1, keepdims=True)
    probs_low = probs.astype(jnp.bfloat16)
    block_out = jnp.einsum("gnqk,knd->qgnd", probs_low.astype(jnp.float32), value_f).astype(jnp.bfloat16)
    row_dot = jnp.sum(grad_f * block_out.astype(jnp.float32), axis=-1)
    grad_probs = jnp.einsum("qgnd,knd->gnqk", grad_f, value_f)
    grad_scores = (probs * (grad_probs - jnp.transpose(row_dot, (1, 2, 0))[..., None]) * softmax_scale).astype(jnp.bfloat16)
    block_dq = jnp.einsum("gnqk,knd->qgnd", grad_scores.astype(jnp.float32), key_f).astype(jnp.bfloat16)
    part_k = jnp.einsum("gnqk,qgnd->knd", grad_scores.astype(jnp.float32), query_f)
    part_v = jnp.einsum("gnqk,qgnd->knd", probs_low.astype(jnp.float32), grad_f)
    return block_out, block_dq, part_k, part_v


def reference(queries, keys, values, output_gradient, selected):
    softmax_scale = HEAD_DIMENSION ** -0.5
    position = jnp.arange(BLK, dtype=jnp.int32)
    causal = position[:, None] >= position[None, :]

    def block_rows(source, block_id):
        return lax.dynamic_slice_in_dim(source, (block_id * BLK).astype(jnp.int32), BLK, 0)

    def one_block(totals, block_id):
        grad_keys, grad_values = totals
        first_pick = selected[block_id, 0]
        second_pick = selected[block_id, 1]
        chosen_blocks = [first_pick, second_pick, block_id]
        block_k = jnp.concatenate([block_rows(keys, chosen) for chosen in chosen_blocks], axis=0)
        block_v = jnp.concatenate([block_rows(values, chosen) for chosen in chosen_blocks], axis=0)
        visible = jnp.concatenate([jnp.broadcast_to(first_pick < block_id, (BLK, BLK)), jnp.broadcast_to(second_pick < block_id, (BLK, BLK)), causal], axis=1)
        block_out, block_dq, part_k, part_v = attend_block(block_rows(queries, block_id), block_k, block_v, block_rows(output_gradient, block_id), visible, softmax_scale)
        for column, chosen in enumerate(chosen_blocks):
            start_row = (chosen * BLK).astype(jnp.int32)
            grad_keys = lax.dynamic_update_slice_in_dim(grad_keys, block_rows(grad_keys, chosen) + part_k[column * BLK:(column + 1) * BLK], start_row, 0)
            grad_values = lax.dynamic_update_slice_in_dim(grad_values, block_rows(grad_values, chosen) + part_v[column * BLK:(column + 1) * BLK], start_row, 0)
        return (grad_keys, grad_values), (block_out, block_dq)

    empty_grads = jnp.zeros(keys.shape, jnp.float32)
    (grad_keys, grad_values), (all_out, all_dq) = lax.scan(one_block, (empty_grads, empty_grads), jnp.arange(NB, dtype=jnp.int32))
    return (all_out.reshape(queries.shape), all_dq.reshape(queries.shape), grad_keys.astype(jnp.bfloat16), grad_values.astype(jnp.bfloat16))
```

```python
import functools
import math

import jax
import jax.numpy as jnp
from jax import lax
from jax.experimental import pallas as pl
from jax.experimental.pallas import tpu as pltpu
from jax.sharding import PartitionSpec as P

F32 = jnp.float32
BF16 = jnp.bfloat16


def dot_nt(a, b):
    return lax.dot_general(a, b, (((1,), (1,)), ((), ())), preferred_element_type=F32)


def dot_nn(a, b):
    return lax.dot_general(a, b, (((1,), (0,)), ((), ())), preferred_element_type=F32)


def attend_kernel(tile, vis_ref, q_ref, do_ref, near_ref, own_ref, out_ref, dq_ref, dnear_ref,
                  down_ref, kt_ref, vt_ref, dk_ref, dv_ref):
    g = pl.program_id(1)
    rows, size = q_ref.shape[2], q_ref.shape[3]
    scale = size ** -0.5
    factor = scale * math.log2(math.e)

    def keys_of(j):
        return near_ref.at[j, 0, 0] if j < 2 else own_ref.at[0, 0]

    def values_of(j):
        return near_ref.at[j, 1, 0] if j < 2 else own_ref.at[1, 0]

    @pl.when(g == 0)
    def _():
        for j in range(3):
            kt_ref[:, j * rows:(j + 1) * rows] = keys_of(j)[...].astype(F32).T.astype(BF16)
            vt_ref[:, j * rows:(j + 1) * rows] = values_of(j)[...].astype(F32).T.astype(BF16)
        dk_ref[...] = jnp.zeros_like(dk_ref)
        dv_ref[...] = jnp.zeros_like(dv_ref)

    for t in range(rows // tile):
        span = slice(t * tile, (t + 1) * tile)
        q = q_ref[0, 0, span, :]
        do = do_ref[0, 0, span, :]
        do_t = do.astype(F32).T
        do_tb = do_t.astype(BF16)
        q_tb = q.astype(F32).T.astype(BF16)
        counts = (rows, rows, (t + 1) * tile)
        scores, tops = [], []
        for j in range(3):
            s = dot_nn(keys_of(j)[0:counts[j], :], q_tb) * factor
            if j == 2:
                key_at = lax.broadcasted_iota(jnp.int32, s.shape, 0)
                query_at = lax.broadcasted_iota(jnp.int32, s.shape, 1) + t * tile
                s = jnp.where(key_at <= query_at, s, -jnp.inf)
            top = jnp.max(s, axis=0, keepdims=True)
            if j < 2:
                top = jnp.where(vis_ref[j] > 0, top, -jnp.inf)
            scores.append(s)
            tops.append(top)
        top = jnp.maximum(jnp.maximum(tops[0], tops[1]), tops[2])
        total = jnp.zeros_like(top)
        weights = []
        for j in range(3):
            shift = jnp.where(vis_ref[j] > 0, top, jnp.inf) if j < 2 else top
            e = jnp.exp2(scores[j] - shift)
            total = total + jnp.sum(e, axis=0, keepdims=True)
            weights.append(e)
        inverse = 1.0 / total
        out_t = jnp.zeros((size, tile), F32)
        lows, probs = [], []
        for j in range(3):
            p = weights[j] * inverse
            low = p.astype(BF16)
            probs.append(p)
            lows.append(low)
            out_t = out_t + dot_nn(vt_ref[:, j * rows:j * rows + counts[j]], low)
        out_low = out_t.astype(BF16).astype(F32)
        out_ref[0, 0, span, :] = out_low.T.astype(BF16)
        row_dot = jnp.sum(do_t * out_low, axis=0, keepdims=True)
        dq_t = jnp.zeros((size, tile), F32)
        for j in range(3):
            dp = dot_nn(values_of(j)[0:counts[j], :], do_tb)
            ds = (probs[j] * (dp - row_dot)).astype(BF16)
            dq_t = dq_t + dot_nn(kt_ref[:, j * rows:j * rows + counts[j]], ds)
            dk_ref[j, 0:counts[j], :] += dot_nn(ds, q)
            dv_ref[j, 0:counts[j], :] += dot_nn(lows[j], do)
        dq_ref[0, 0, span, :] = (dq_t * scale).T.astype(BF16)

    @pl.when(g == pl.num_programs(1) - 1)
    def _():
        for j in range(2):
            dnear_ref[j, 0, 0] = (dk_ref[j] * scale).astype(BF16)
            dnear_ref[j, 1, 0] = dv_ref[j].astype(BF16)
        down_ref[0, 0] = dk_ref[2] * scale
        down_ref[1, 0] = dv_ref[2]


def attend(visible, q, do, near, own):
    heads, group, rows, size = q.shape
    tile = min(256, rows)
    head_spec = pl.BlockSpec((1, 1, rows, size), lambda n, g, *_: (n, g, 0, 0))
    near_spec = pl.BlockSpec((2, 2, 1, rows, size), lambda n, g, *_: (0, 0, n, 0, 0))
    own_spec = pl.BlockSpec((2, 1, rows, size), lambda n, g, *_: (0, n, 0, 0))
    return pl.pallas_call(
        functools.partial(attend_kernel, tile),
        grid_spec=pltpu.PrefetchScalarGridSpec(
            num_scalar_prefetch=1,
            grid=(heads, group),
            in_specs=[head_spec, head_spec, near_spec, own_spec],
            out_specs=[head_spec, head_spec, near_spec, own_spec],
            scratch_shapes=[
                pltpu.VMEM((size, 3 * rows), BF16),
                pltpu.VMEM((size, 3 * rows), BF16),
                pltpu.VMEM((3, rows, size), F32),
                pltpu.VMEM((3, rows, size), F32),
            ],
        ),
        out_shape=[
            jax.ShapeDtypeStruct(q.shape, BF16),
            jax.ShapeDtypeStruct(q.shape, BF16),
            jax.ShapeDtypeStruct(near.shape, BF16),
            jax.ShapeDtypeStruct(own.shape, F32),
        ],
        compiler_params=pltpu.CompilerParams(vmem_limit_bytes=56 * 2**20),
    )(visible, q, do, near, own)


def on_device(queries, keys, values, output_gradient, selected):
    rows, kv_count, size = keys.shape
    blocks = lax.axis_size("ctx")
    own_heads = kv_count // lax.axis_size("head")
    me = lax.axis_index("ctx")
    half = lax.axis_index("head")

    def to_heads(x):
        x = lax.all_to_all(x, "head", split_axis=2, concat_axis=1, tiled=True)
        return jnp.transpose(x, (2, 1, 0, 3))

    def from_heads(x):
        x = jnp.transpose(x, (2, 1, 0, 3))
        return lax.all_to_all(x, "head", split_axis=1, concat_axis=2, tiled=True)

    q, do = to_heads(queries), to_heads(output_gradient)
    own = jnp.stack([keys, values])
    own = lax.dynamic_slice_in_dim(own, half * own_heads, own_heads, 2)
    own = jnp.transpose(own, (0, 2, 1, 3))
    piece = 2 * own_heads * rows // blocks
    flat = own.reshape(blocks, piece, size)
    held = lax.all_to_all(flat, "ctx", split_axis=0, concat_axis=0, tiled=True)
    near = lax.all_to_all(held[jnp.transpose(selected)], "ctx", split_axis=1, concat_axis=1, tiled=True)
    near = near.reshape((2,) + own.shape)
    visible = (lax.dynamic_index_in_dim(selected, me, 0, keepdims=False) < me).astype(jnp.int32)
    out, dq, dnear, down = attend(visible, q, do, near, own)
    back = lax.all_to_all(dnear.reshape(2, blocks, piece, size), "ctx", split_axis=1, concat_axis=1, tiled=True)
    owners = (jnp.transpose(selected)[:, :, None] == jnp.arange(blocks, dtype=jnp.int32)).astype(BF16)
    home = jnp.einsum("jrb,jrpd->bpd", owners, back, preferred_element_type=F32).astype(BF16)
    home = lax.all_to_all(home, "ctx", split_axis=0, concat_axis=0, tiled=True)
    grads = (home.reshape(own.shape).astype(F32) + down).astype(BF16)
    grads = jnp.transpose(grads, (0, 2, 1, 3))
    return from_heads(out), from_heads(dq), grads[0], grads[1]


def solution(mesh):
    return jax.shard_map(
        on_device,
        mesh=mesh,
        in_specs=(
            P("ctx", "head", None, None),
            P("ctx", None, None),
            P("ctx", None, None),
            P("ctx", "head", None, None),
            P(),
        ),
        out_specs=(
            P("ctx", "head", None, None),
            P("ctx", "head", None, None),
            P("ctx", "head", None),
            P("ctx", "head", None),
        ),
        check_vma=False,
    )
```

```python
import functools
import math

import jax
import jax.numpy as jnp
from jax import lax
from jax.experimental import pallas as pl
from jax.experimental.pallas import tpu as pltpu
from jax.sharding import PartitionSpec as P

F32 = jnp.float32
BF16 = jnp.bfloat16


def dot_nt(a, b):
    return lax.dot_general(a, b, (((1,), (1,)), ((), ())), preferred_element_type=F32)


def dot_nn(a, b):
    return lax.dot_general(a, b, (((1,), (0,)), ((), ())), preferred_element_type=F32)


def attend_kernel(tile, vis_ref, q_ref, do_ref, near_ref, own_ref, out_ref, dq_ref, dnear_ref,
                  down_ref, kt_ref, vt_ref, dk_ref, dv_ref):
    g = pl.program_id(1)
    rows, size = q_ref.shape[2], q_ref.shape[3]
    scale = size ** -0.5
    factor = scale * math.log2(math.e)

    def keys_of(j):
        return near_ref.at[0, j, 0] if j < 2 else own_ref.at[0, 0]

    def values_of(j):
        return near_ref.at[0, j, 1] if j < 2 else own_ref.at[0, 1]

    @pl.when(g == 0)
    def _():
        for j in range(3):
            kt_ref[:, j * rows:(j + 1) * rows] = keys_of(j)[...].astype(F32).T.astype(BF16)
            vt_ref[:, j * rows:(j + 1) * rows] = values_of(j)[...].astype(F32).T.astype(BF16)
        dk_ref[...] = jnp.zeros_like(dk_ref)
        dv_ref[...] = jnp.zeros_like(dv_ref)

    for t in range(rows // tile):
        span = slice(t * tile, (t + 1) * tile)
        q = q_ref[0, 0, span, :]
        do = do_ref[0, 0, span, :]
        do_t = do.astype(F32).T
        do_tb = do_t.astype(BF16)
        q_tb = q.astype(F32).T.astype(BF16)
        counts = (rows, rows, (t + 1) * tile)
        scores, tops = [], []
        for j in range(3):
            s = dot_nn(keys_of(j)[0:counts[j], :], q_tb) * factor
            if j == 2:
                key_at = lax.broadcasted_iota(jnp.int32, s.shape, 0)
                query_at = lax.broadcasted_iota(jnp.int32, s.shape, 1) + t * tile
                s = jnp.where(key_at <= query_at, s, -jnp.inf)
            top = jnp.max(s, axis=0, keepdims=True)
            if j < 2:
                top = jnp.where(vis_ref[j] > 0, top, -jnp.inf)
            scores.append(s)
            tops.append(top)
        top = jnp.maximum(jnp.maximum(tops[0], tops[1]), tops[2])
        total = jnp.zeros_like(top)
        weights = []
        for j in range(3):
            shift = jnp.where(vis_ref[j] > 0, top, jnp.inf) if j < 2 else top
            e = jnp.exp2(scores[j] - shift)
            total = total + jnp.sum(e, axis=0, keepdims=True)
            weights.append(e)
        inverse = 1.0 / total
        out_t = jnp.zeros((size, tile), F32)
        lows, probs = [], []
        for j in range(3):
            p = weights[j] * inverse
            low = p.astype(BF16)
            probs.append(p)
            lows.append(low)
            out_t = out_t + dot_nn(vt_ref[:, j * rows:j * rows + counts[j]], low)
        out_low = out_t.astype(BF16).astype(F32)
        out_ref[0, 0, span, :] = out_low.T.astype(BF16)
        row_dot = jnp.sum(do_t * out_low, axis=0, keepdims=True)
        dq_t = jnp.zeros((size, tile), F32)
        for j in range(3):
            dp = dot_nn(values_of(j)[0:counts[j], :], do_tb)
            ds = (probs[j] * (dp - row_dot)).astype(BF16)
            dq_t = dq_t + dot_nn(kt_ref[:, j * rows:j * rows + counts[j]], ds)
            dk_ref[j, 0:counts[j], :] += dot_nn(ds, q)
            dv_ref[j, 0:counts[j], :] += dot_nn(lows[j], do)
        dq_ref[0, 0, span, :] = (dq_t * scale).T.astype(BF16)

    @pl.when(g == pl.num_programs(1) - 1)
    def _():
        for j in range(2):
            dnear_ref[0, j, 0] = (dk_ref[j] * scale).astype(BF16)
            dnear_ref[0, j, 1] = dv_ref[j].astype(BF16)
        down_ref[0, 0] = dk_ref[2] * scale
        down_ref[0, 1] = dv_ref[2]


def attend(visible, q, do, near, own):
    heads, group, rows, size = q.shape
    tile = min(256, rows)
    head_spec = pl.BlockSpec((1, 1, rows, size), lambda n, g, *_: (n, g, 0, 0))
    near_spec = pl.BlockSpec((1, 2, 2, rows, size), lambda n, g, *_: (n, 0, 0, 0, 0))
    own_spec = pl.BlockSpec((1, 2, rows, size), lambda n, g, *_: (n, 0, 0, 0))
    return pl.pallas_call(
        functools.partial(attend_kernel, tile),
        grid_spec=pltpu.PrefetchScalarGridSpec(
            num_scalar_prefetch=1,
            grid=(heads, group),
            in_specs=[head_spec, head_spec, near_spec, own_spec],
            out_specs=[head_spec, head_spec, near_spec, own_spec],
            scratch_shapes=[
                pltpu.VMEM((size, 3 * rows), BF16),
                pltpu.VMEM((size, 3 * rows), BF16),
                pltpu.VMEM((3, rows, size), F32),
                pltpu.VMEM((3, rows, size), F32),
            ],
        ),
        out_shape=[
            jax.ShapeDtypeStruct(q.shape, BF16),
            jax.ShapeDtypeStruct(q.shape, BF16),
            jax.ShapeDtypeStruct(near.shape, BF16),
            jax.ShapeDtypeStruct(own.shape, F32),
        ],
        compiler_params=pltpu.CompilerParams(vmem_limit_bytes=56 * 2**20),
    )(visible, q, do, near, own)


def greet(blocks, halves):
    me, half = lax.axis_index("ctx"), lax.axis_index("head")
    barrier = pltpu.get_barrier_semaphore()

    @pl.loop(1, blocks)
    def _(i):
        pl.semaphore_signal(barrier, inc=1, device_id={"ctx": lax.rem(me + i, blocks), "head": half})

    for i in range(1, halves):
        pl.semaphore_signal(barrier, inc=1, device_id={"ctx": me, "head": lax.rem(half + i, halves)})
    pl.semaphore_wait(barrier, blocks - 1 + halves - 1)


def fetch_kernel(blocks, halves, sel_ref, kv_ref, q_ref, do_ref, near_ref, qo_ref, doo_ref,
                 send, stage, s1, r1, s2, r2, local2, xs, xr, xl, *held):
    me, half = lax.axis_index("ctx"), lax.axis_index("head")
    heads = kv_ref.shape[0]
    part = q_ref.shape[1]
    greet(blocks, halves)

    for n in range(heads):
        @pl.loop(1, blocks)
        def _(i):
            peer = lax.rem(me + i, blocks)
            pltpu.make_async_remote_copy(
                kv_ref.at[n, peer], held[n].at[me], s1.at[n], r1.at[n],
                device_id={"ctx": peer, "head": half}).start()

    pairs = ((q_ref, qo_ref), (do_ref, doo_ref))
    moves = []
    for e, (src, dst) in enumerate(pairs):
        place = dst.at[:, pl.ds(half * part, part)]
        for i in range(1, halves):
            other = lax.rem(half + i, halves)
            move = pltpu.make_async_remote_copy(
                src.at[pl.ds(other * heads, heads)], place, xs.at[e, i - 1], xr.at[e, i - 1],
                device_id={"ctx": me, "head": other})
            move.start()
            moves.append(move)
        pltpu.make_async_copy(src.at[pl.ds(half * heads, heads)], stage.at[e], xl.at[e]).start()

    for n in range(heads):
        held[n][me] = kv_ref[n, me]

    for e, (src, dst) in enumerate(pairs):
        pltpu.make_async_copy(src.at[pl.ds(half * heads, heads)], stage.at[e], xl.at[e]).wait()
        pltpu.make_async_copy(stage.at[e], dst.at[:, pl.ds(half * part, part)], xl.at[e]).start()

    for n in range(heads):
        pltpu.make_async_remote_copy(
            kv_ref.at[n, pl.ds(0, blocks - 1)], held[n].at[pl.ds(0, blocks - 1)], s1.at[n], r1.at[n],
            device_id={"ctx": me, "head": half}).wait_recv()

        @pl.loop(0, blocks)
        def _(dest):
            for j in range(2):
                send[n, dest, j] = held[n][sel_ref[dest, j]]

        @pl.loop(1, blocks)
        def _(i):
            dest = lax.rem(me + i, blocks)
            pltpu.make_async_remote_copy(
                send.at[n, dest], near_ref.at[n, :, me], s2.at[n], r2.at[n],
                device_id={"ctx": dest, "head": half}).start()

        pltpu.make_async_copy(send.at[n, me], near_ref.at[n, :, me], local2.at[n]).start()

    for n in range(heads):
        pltpu.make_async_copy(send.at[n, me], near_ref.at[n, :, me], local2.at[n]).wait()
        done1 = pltpu.make_async_remote_copy(
            kv_ref.at[n, pl.ds(0, blocks - 1)], held[n].at[pl.ds(0, blocks - 1)], s1.at[n], r1.at[n],
            device_id={"ctx": me, "head": half})
        done1.wait_send()
        done2 = pltpu.make_async_remote_copy(
            send.at[n, pl.ds(0, blocks - 1)], near_ref.at[n, :, pl.ds(0, blocks - 1)], s2.at[n], r2.at[n],
            device_id={"ctx": me, "head": half})
        done2.wait_send()
        done2.wait_recv()
    for move in moves:
        move.wait()
    for e, (src, dst) in enumerate(pairs):
        pltpu.make_async_copy(stage.at[e], dst.at[:, pl.ds(half * part, part)], xl.at[e]).wait()


def fetch(selected, kv, q, do, blocks, halves):
    heads, _, piece, size = kv.shape
    full, part, rows, _ = q.shape
    whole = pl.BlockSpec(memory_space=pltpu.VMEM)
    far = pl.BlockSpec(memory_space=pl.ANY)
    mixed = jax.ShapeDtypeStruct((heads, part * halves, rows, size), BF16)
    dma = pltpu.SemaphoreType.DMA
    return pl.pallas_call(
        functools.partial(fetch_kernel, blocks, halves),
        in_specs=[pl.BlockSpec(memory_space=pltpu.SMEM), whole, far, far],
        out_specs=[far, far, far],
        out_shape=[jax.ShapeDtypeStruct((heads, 2, blocks, piece, size), BF16), mixed, mixed],
        scratch_shapes=[
            pltpu.VMEM((heads, blocks, 2, piece, size), BF16),
            pltpu.VMEM((2, heads, part, rows, size), BF16),
            dma((heads,)), dma((heads,)), dma((heads,)), dma((heads,)), dma((heads,)),
            dma((2, halves - 1)), dma((2, halves - 1)), dma((2,)),
        ] + [pltpu.VMEM((blocks, piece, size), BF16)] * heads,
        compiler_params=pltpu.CompilerParams(collective_id=0, has_side_effects=True,
                                             vmem_limit_bytes=32 * 2**20),
    )(selected, kv, q, do)


def return_kernel(blocks, halves, sel_ref, dnear_ref, out_ref, dq_ref, ret_ref, oo_ref, dqo_ref,
                  arrived, home, stage, s1, r1, s2, r2, local1, local2, xs, xr, xl):
    me, half = lax.axis_index("ctx"), lax.axis_index("head")
    heads = dnear_ref.shape[0]
    part = out_ref.shape[1] // halves
    greet(blocks, halves)

    def own_first(n):
        return pltpu.make_async_copy(dnear_ref.at[n, :, me], arrived.at[n, me], local1.at[n])

    def own_last(n):
        return pltpu.make_async_copy(home.at[n, me], ret_ref.at[n, me], local2.at[n])

    for n in range(heads):
        @pl.loop(1, blocks)
        def _(i):
            peer = lax.rem(me + i, blocks)
            pltpu.make_async_remote_copy(
                dnear_ref.at[n, :, peer], arrived.at[n, me], s1.at[n], r1.at[n],
                device_id={"ctx": peer, "head": half}).start()

        own_first(n).start()

    pairs = ((out_ref, oo_ref), (dq_ref, dqo_ref))
    moves = []
    for e, (src, dst) in enumerate(pairs):
        place = dst.at[pl.ds(half * heads, heads)]
        for i in range(1, halves):
            other = lax.rem(half + i, halves)
            move = pltpu.make_async_remote_copy(
                src.at[:, pl.ds(other * part, part)], place, xs.at[e, i - 1], xr.at[e, i - 1],
                device_id={"ctx": me, "head": other})
            move.start()
            moves.append(move)
        pltpu.make_async_copy(src.at[:, pl.ds(half * part, part)], stage.at[e], xl.at[e]).start()
    for e, (src, dst) in enumerate(pairs):
        pltpu.make_async_copy(src.at[:, pl.ds(half * part, part)], stage.at[e], xl.at[e]).wait()
        pltpu.make_async_copy(stage.at[e], dst.at[pl.ds(half * heads, heads)], xl.at[e]).start()

    def first(n):
        return pltpu.make_async_remote_copy(
            dnear_ref.at[n, :, pl.ds(0, blocks - 1)], arrived.at[n, pl.ds(0, blocks - 1)], s1.at[n], r1.at[n],
            device_id={"ctx": me, "head": half})

    def last(n):
        return pltpu.make_async_remote_copy(
            home.at[n, pl.ds(0, blocks - 1)], ret_ref.at[n, pl.ds(0, blocks - 1)], s2.at[n], r2.at[n],
            device_id={"ctx": me, "head": half})

    for n in range(heads):
        first(n).wait_recv()
        own_first(n).wait()

        @pl.loop(0, blocks)
        def _(s):
            def add(b, total):
                for j in range(2):
                    mine = (sel_ref[b, j] == s).astype(F32)
                    total = total + arrived[n, b, j].astype(F32) * mine
                return total

            total = lax.fori_loop(s, blocks, add, jnp.zeros(home.shape[2:], F32))
            home[n, s] = total.astype(BF16)

        @pl.loop(1, blocks)
        def _(i):
            dest = lax.rem(me + i, blocks)
            pltpu.make_async_remote_copy(
                home.at[n, dest], ret_ref.at[n, me], s2.at[n], r2.at[n],
                device_id={"ctx": dest, "head": half}).start()

        own_last(n).start()

    for n in range(heads):
        own_last(n).wait()
        first(n).wait_send()
        last(n).wait_send()
        last(n).wait_recv()
    for move in moves:
        move.wait()
    for e, (src, dst) in enumerate(pairs):
        pltpu.make_async_copy(stage.at[e], dst.at[pl.ds(half * heads, heads)], xl.at[e]).wait()


def give_back(selected, dnear, out, dq, blocks, halves):
    heads, _, _, piece, size = dnear.shape
    _, group, rows, _ = out.shape
    far = pl.BlockSpec(memory_space=pl.ANY)
    mixed = jax.ShapeDtypeStruct((heads * halves, group // halves, rows, size), BF16)
    dma = pltpu.SemaphoreType.DMA
    return pl.pallas_call(
        functools.partial(return_kernel, blocks, halves),
        in_specs=[pl.BlockSpec(memory_space=pltpu.SMEM), far, far, far],
        out_specs=[far, far, far],
        out_shape=[jax.ShapeDtypeStruct((heads, blocks, piece, size), BF16), mixed, mixed],
        scratch_shapes=[
            pltpu.VMEM((heads, blocks, 2, piece, size), BF16),
            pltpu.VMEM((heads, blocks, piece, size), BF16),
            pltpu.VMEM((2, heads, group // halves, rows, size), BF16),
            dma((heads,)), dma((heads,)), dma((heads,)), dma((heads,)), dma((heads,)), dma((heads,)),
            dma((2, halves - 1)), dma((2, halves - 1)), dma((2,)),
        ],
        compiler_params=pltpu.CompilerParams(collective_id=1, has_side_effects=True,
                                             vmem_limit_bytes=32 * 2**20),
    )(selected, dnear, out, dq)


def on_device(queries, keys, values, output_gradient, selected):
    rows, kv_count, size = keys.shape
    blocks, halves = lax.axis_size("ctx"), lax.axis_size("head")
    own_heads = kv_count // halves
    me = lax.axis_index("ctx")
    half = lax.axis_index("head")
    piece = 2 * rows // blocks
    own = jnp.stack([keys, values])
    own = lax.dynamic_slice_in_dim(own, half * own_heads, own_heads, 2)
    own = jnp.transpose(own, (2, 0, 1, 3))
    q, do = jnp.transpose(queries, (2, 1, 0, 3)), jnp.transpose(output_gradient, (2, 1, 0, 3))
    near, q, do = fetch(selected, own.reshape(own_heads, blocks, piece, size), q, do, blocks, halves)
    near = near.reshape(own_heads, 2, 2, rows, size)
    visible = (lax.dynamic_index_in_dim(selected, me, 0, keepdims=False) < me).astype(jnp.int32)
    out, dq, dnear, down = attend(visible, q, do, near, own)
    ret, out, dq = give_back(
        selected, dnear.reshape(own_heads, 2, blocks, piece, size), out, dq, blocks, halves)
    grads = (ret.reshape(own.shape).astype(F32) + down).astype(BF16)
    grads = jnp.transpose(grads, (1, 2, 0, 3))
    return jnp.transpose(out, (2, 1, 0, 3)), jnp.transpose(dq, (2, 1, 0, 3)), grads[0], grads[1]


def solution(mesh):
    return jax.shard_map(
        on_device,
        mesh=mesh,
        in_specs=(
            P("ctx", "head", None, None),
            P("ctx", None, None),
            P("ctx", None, None),
            P("ctx", "head", None, None),
            P(),
        ),
        out_specs=(
            P("ctx", "head", None, None),
            P("ctx", "head", None, None),
            P("ctx", "head", None),
            P("ctx", "head", None),
        ),
        check_vma=False,
    )
```

```python
import functools
import math

import jax
import jax.numpy as jnp
from jax import lax
from jax.experimental import pallas as pl
from jax.experimental.pallas import tpu as pltpu
from jax.sharding import PartitionSpec as P

F32 = jnp.float32
BF16 = jnp.bfloat16


def dot_nt(a, b):
    return lax.dot_general(a, b, (((1,), (1,)), ((), ())), preferred_element_type=F32)


def dot_nn(a, b):
    return lax.dot_general(a, b, (((1,), (0,)), ((), ())), preferred_element_type=F32)


def greet(blocks, halves):
    me, half = lax.axis_index("ctx"), lax.axis_index("head")
    barrier = pltpu.get_barrier_semaphore()

    @pl.loop(1, blocks)
    def _(i):
        pl.semaphore_signal(barrier, inc=1, device_id={"ctx": lax.rem(me + i, blocks), "head": half})

    for i in range(1, halves):
        pl.semaphore_signal(barrier, inc=1, device_id={"ctx": me, "head": lax.rem(half + i, halves)})
    pl.semaphore_wait(barrier, blocks - 1 + halves - 1)


def attend_tile(t, tile, scale, visible, q, do, keys, values, kt_ref, vt_ref, dk_ref, dv_ref):
    rows, size = keys.shape[1], keys.shape[2]
    factor = scale * math.log2(math.e)
    do_t = do.astype(F32).T
    do_tb = do_t.astype(BF16)
    q_tb = q.astype(F32).T.astype(BF16)
    counts = (rows, rows, (t + 1) * tile)
    scores, tops = [], []
    for j in range(3):
        s = dot_nn(keys[j, 0:counts[j], :], q_tb) * factor
        if j == 2:
            key_at = lax.broadcasted_iota(jnp.int32, s.shape, 0)
            query_at = lax.broadcasted_iota(jnp.int32, s.shape, 1) + t * tile
            s = jnp.where(key_at <= query_at, s, -jnp.inf)
        top = jnp.max(s, axis=0, keepdims=True)
        if j < 2:
            top = jnp.where(visible[j], top, -jnp.inf)
        scores.append(s)
        tops.append(top)
    top = jnp.maximum(jnp.maximum(tops[0], tops[1]), tops[2])
    total = jnp.zeros_like(top)
    weights = []
    for j in range(3):
        shift = jnp.where(visible[j], top, jnp.inf) if j < 2 else top
        e = jnp.exp2(scores[j] - shift)
        total = total + jnp.sum(e, axis=0, keepdims=True)
        weights.append(e)
    inverse = 1.0 / total
    out_t = jnp.zeros((size, tile), F32)
    lows, probs = [], []
    for j in range(3):
        p = weights[j] * inverse
        low = p.astype(BF16)
        probs.append(p)
        lows.append(low)
        out_t = out_t + dot_nn(vt_ref[:, j * rows:j * rows + counts[j]], low)
    out_low = out_t.astype(BF16).astype(F32)
    row_dot = jnp.sum(do_t * out_low, axis=0, keepdims=True)
    dq_t = jnp.zeros((size, tile), F32)
    for j in range(3):
        dp = dot_nn(values[j, 0:counts[j], :], do_tb)
        ds = (probs[j] * (dp - row_dot)).astype(BF16)
        dq_t = dq_t + dot_nn(kt_ref[:, j * rows:j * rows + counts[j]], ds)
        dk_ref[j, 0:counts[j], :] += dot_nn(ds, q)
        dv_ref[j, 0:counts[j], :] += dot_nn(lows[j], do)
    return out_low.T.astype(BF16), (dq_t * scale).T.astype(BF16)


def step_kernel(blocks, halves, tile, sel_ref, kv_ref, own_ref, q_ref, do_ref, grads_ref, oo_ref, dqo_ref,
                qv, dov, near, send, ks, vs, kt, vt, dk, dv, down, outv, dqv, dnear, arrived, home, ret,
                s1, r1, s2, r2, xs, xr, xl, b1, c1, b2, c2, ys, yr, yl, *held):
    me, half = lax.axis_index("ctx"), lax.axis_index("head")
    heads, group, rows, size = qv.shape
    part = group // halves
    piece = kv_ref.shape[2]
    scale = size ** -0.5
    visible = [sel_ref[me, j] < me for j in range(2)]
    here = {"ctx": me, "head": half}
    greet(blocks, halves)

    def send_all(make):
        @pl.loop(1, blocks)
        def _(i):
            make(lax.rem(me + i, blocks)).start()

    for n in range(heads):
        send_all(lambda peer: pltpu.make_async_remote_copy(
            kv_ref.at[n, peer], held[n].at[me], s1.at[n], r1.at[n], device_id={"ctx": peer, "head": half}))

    moves = []
    for e, (src, dst) in enumerate(((q_ref, qv), (do_ref, dov))):
        place = dst.at[:, pl.ds(half * part, part)]
        for i in range(1, halves):
            other = lax.rem(half + i, halves)
            moves.append(pltpu.make_async_remote_copy(
                src.at[pl.ds(other * heads, heads)], place, xs.at[e, i - 1], xr.at[e, i - 1],
                device_id={"ctx": me, "head": other}))
        moves.append(pltpu.make_async_copy(src.at[pl.ds(half * heads, heads)], place, xl.at[e]))
    for move in moves:
        move.start()

    def fetch_first(n):
        return pltpu.make_async_remote_copy(
            kv_ref.at[n, pl.ds(0, blocks - 1)], held[n].at[pl.ds(0, blocks - 1)], s1.at[n], r1.at[n],
            device_id=here)

    def fetch_last(n):
        return pltpu.make_async_remote_copy(
            send.at[n, pl.ds(0, blocks - 1)], near.at[n, :, pl.ds(0, blocks - 1)], s2.at[n], r2.at[n],
            device_id=here)

    for n in range(heads):
        held[n][me] = kv_ref[n, me]
        fetch_first(n).wait_recv()

        @pl.loop(0, blocks)
        def _(dest):
            for j in range(2):
                send[n, dest, j] = held[n][sel_ref[dest, j]]

        send_all(lambda dest: pltpu.make_async_remote_copy(
            send.at[n, dest], near.at[n, :, me], s2.at[n], r2.at[n], device_id={"ctx": dest, "head": half}))
        for j in range(2):
            near[n, j, me] = held[n][sel_ref[me, j]]

    for move in moves:
        move.wait()

    def back_first(n):
        return pltpu.make_async_remote_copy(
            dnear.at[n, :, pl.ds(0, blocks - 1)], arrived.at[n, pl.ds(0, blocks - 1)], b1.at[n], c1.at[n],
            device_id=here)

    def back_last(n):
        return pltpu.make_async_remote_copy(
            home.at[n, pl.ds(0, blocks - 1)], ret.at[n, pl.ds(0, blocks - 1)], b2.at[n], c2.at[n],
            device_id=here)

    def collect(n):
        back_first(n).wait_recv()

        @pl.loop(0, blocks)
        def _(s):
            def add(b, total):
                for j in range(2):
                    mine = (sel_ref[b, j] == s).astype(F32)
                    total = total + arrived[n, b, j].astype(F32) * mine
                return total

            total = lax.fori_loop(s, blocks, add, jnp.zeros((piece, size), F32))
            home[n, s] = total.astype(BF16)

        send_all(lambda dest: pltpu.make_async_remote_copy(
            home.at[n, dest], ret.at[n, me], b2.at[n], c2.at[n], device_id={"ctx": dest, "head": half}))
        ret[n, me] = home[n, me]

    def results(n):
        made = []
        for e, (src, dst) in enumerate(((outv, oo_ref), (dqv, dqo_ref))):
            place = dst.at[half * heads + n]
            for i in range(1, halves):
                other = lax.rem(half + i, halves)
                made.append(pltpu.make_async_remote_copy(
                    src.at[n, pl.ds(other * part, part)], place, ys.at[n, e, i - 1], yr.at[n, e, i - 1],
                    device_id={"ctx": me, "head": other}))
            made.append(pltpu.make_async_copy(src.at[n, pl.ds(half * part, part)], place, yl.at[n, e]))
        return made

    def join(x):
        if piece % 16 == 0:
            return x.reshape(rows, size)
        return x.astype(F32).reshape(rows, size).astype(BF16)

    pieces = blocks // 2

    @pl.loop(0, heads * group)
    def _(at):
        n = at // group
        g = at % group

        @pl.when(g == 0)
        def _():
            fetch_last(n).wait_recv()
            for j in range(3):
                if j < 2:
                    k, v = join(near[n, j, 0:pieces]), join(near[n, j, pieces:2 * pieces])
                else:
                    k, v = own_ref[n, 0], own_ref[n, 1]
                ks[j] = k
                vs[j] = v
                kt[:, j * rows:(j + 1) * rows] = k.astype(F32).T.astype(BF16)
                vt[:, j * rows:(j + 1) * rows] = v.astype(F32).T.astype(BF16)
            dk[...] = jnp.zeros_like(dk)
            dv[...] = jnp.zeros_like(dv)

        for t in range(rows // tile):
            span = slice(t * tile, (t + 1) * tile)
            out, dq = attend_tile(t, tile, scale, visible, qv[n, g, span, :], dov[n, g, span, :],
                                  ks, vs, kt, vt, dk, dv)
            outv[n, g, span, :] = out
            dqv[n, g, span, :] = dq

        @pl.when(g == group - 1)
        def _():
            for j in range(2):
                dnear[n, j, 0:pieces] = (dk[j] * scale).reshape(pieces, piece, size).astype(BF16)
                dnear[n, j, pieces:2 * pieces] = dv[j].reshape(pieces, piece, size).astype(BF16)
            down[n, 0:pieces] = (dk[2] * scale).reshape(pieces, piece, size)
            down[n, pieces:2 * pieces] = dv[2].reshape(pieces, piece, size)
            send_all(lambda peer: pltpu.make_async_remote_copy(
                dnear.at[n, :, peer], arrived.at[n, me], b1.at[n], c1.at[n],
                device_id={"ctx": peer, "head": half}))
            for j in range(2):
                arrived[n, me, j] = dnear[n, j, me]
            for move in results(n):
                move.start()

        @pl.when((n > 0) & (g == group - 2))
        def _():
            collect(n - 1)

    collect(heads - 1)
    for n in range(heads):
        fetch_first(n).wait_send()
        fetch_last(n).wait_send()
        back_first(n).wait_send()
        for move in results(n):
            move.wait()
    for n in range(heads):
        back_last(n).wait_send()
        back_last(n).wait_recv()
        grads_ref[n] = (ret[n].astype(F32) + down[n]).astype(BF16)


def step(selected, kv, own, q, do, blocks, halves):
    heads, _, piece, size = kv.shape
    full, part, rows, _ = q.shape
    group = part * halves
    tile = min(256, rows)
    near = pl.BlockSpec(memory_space=pltpu.VMEM)
    far = pl.BlockSpec(memory_space=pl.ANY)
    dma = pltpu.SemaphoreType.DMA
    vmem = pltpu.VMEM
    return pl.pallas_call(
        functools.partial(step_kernel, blocks, halves, tile),
        in_specs=[pl.BlockSpec(memory_space=pltpu.SMEM), near, near, far, far],
        out_specs=[near, far, far],
        out_shape=[jax.ShapeDtypeStruct(kv.shape, BF16), jax.ShapeDtypeStruct(q.shape, BF16),
                   jax.ShapeDtypeStruct(q.shape, BF16)],
        scratch_shapes=[
            vmem((heads, group, rows, size), BF16),
            vmem((heads, group, rows, size), BF16),
            vmem((heads, 2, blocks, piece, size), BF16),
            vmem((heads, blocks, 2, piece, size), BF16),
            vmem((3, rows, size), BF16),
            vmem((3, rows, size), BF16),
            vmem((size, 3 * rows), BF16),
            vmem((size, 3 * rows), BF16),
            vmem((3, rows, size), F32),
            vmem((3, rows, size), F32),
            vmem((heads, blocks, piece, size), F32),
            vmem((heads, group, rows, size), BF16),
            vmem((heads, group, rows, size), BF16),
            vmem((heads, 2, blocks, piece, size), BF16),
            vmem((heads, blocks, 2, piece, size), BF16),
            vmem((heads, blocks, piece, size), BF16),
            vmem((heads, blocks, piece, size), BF16),
            dma((heads,)), dma((heads,)), dma((heads,)), dma((heads,)),
            dma((2, halves - 1)), dma((2, halves - 1)), dma((2,)),
            dma((heads,)), dma((heads,)), dma((heads,)), dma((heads,)),
            dma((heads, 2, halves - 1)), dma((heads, 2, halves - 1)), dma((heads, 2)),
        ] + [vmem((blocks, piece, size), BF16)] * heads,
        compiler_params=pltpu.CompilerParams(collective_id=0, has_side_effects=True,
                                             vmem_limit_bytes=56 * 2**20),
    )(selected, kv, own, q, do)


def on_device(queries, keys, values, output_gradient, selected):
    rows, kv_count, size = keys.shape
    blocks, halves = lax.axis_size("ctx"), lax.axis_size("head")
    own_heads = kv_count // halves
    half = lax.axis_index("head")
    piece = 2 * rows // blocks
    own = jnp.stack([keys, values])
    own = lax.dynamic_slice_in_dim(own, half * own_heads, own_heads, 2)
    own = jnp.transpose(own, (2, 0, 1, 3))
    q, do = jnp.transpose(queries, (2, 1, 0, 3)), jnp.transpose(output_gradient, (2, 1, 0, 3))
    grads, out, dq = step(selected, own.reshape(own_heads, blocks, piece, size), own, q, do, blocks, halves)
    grads = jnp.transpose(grads.reshape(own.shape), (1, 2, 0, 3))
    return jnp.transpose(out, (2, 1, 0, 3)), jnp.transpose(dq, (2, 1, 0, 3)), grads[0], grads[1]


def solution(mesh):
    return jax.shard_map(
        on_device,
        mesh=mesh,
        in_specs=(
            P("ctx", "head", None, None),
            P("ctx", None, None),
            P("ctx", None, None),
            P("ctx", "head", None, None),
            P(),
        ),
        out_specs=(
            P("ctx", "head", None, None),
            P("ctx", "head", None, None),
            P("ctx", "head", None),
            P("ctx", "head", None),
        ),
        check_vma=False,
    )
```

```python
import functools
import math

import jax
import jax.numpy as jnp
from jax import lax
from jax.experimental import pallas as pl
from jax.experimental.pallas import tpu as pltpu
from jax.sharding import PartitionSpec as P

F32 = jnp.float32
BF16 = jnp.bfloat16


def dot_nt(a, b):
    return lax.dot_general(a, b, (((1,), (1,)), ((), ())), preferred_element_type=F32)


def dot_nn(a, b):
    return lax.dot_general(a, b, (((1,), (0,)), ((), ())), preferred_element_type=F32)


def greet(blocks, halves):
    me, half = lax.axis_index("ctx"), lax.axis_index("head")
    barrier = pltpu.get_barrier_semaphore()

    @pl.loop(1, blocks)
    def _(i):
        pl.semaphore_signal(barrier, inc=1, device_id={"ctx": lax.rem(me + i, blocks), "head": half})

    for i in range(1, halves):
        pl.semaphore_signal(barrier, inc=1, device_id={"ctx": me, "head": lax.rem(half + i, halves)})
    pl.semaphore_wait(barrier, blocks - 1 + halves - 1)


def attend_tile(t, tile, scale, visible, q, do, keys, values, kt_ref, vt_ref, dk_ref, dv_ref):
    rows, size = keys.shape[1], keys.shape[2]
    factor = scale * math.log2(math.e)
    do_t = do.astype(F32).T
    do_tb = do_t.astype(BF16)
    q_tb = q.astype(F32).T.astype(BF16)
    counts = (rows, rows, (t + 1) * tile)
    scores, tops = [], []
    for j in range(3):
        s = dot_nn(keys[j, 0:counts[j], :], q_tb) * factor
        if j == 2:
            key_at = lax.broadcasted_iota(jnp.int32, s.shape, 0)
            query_at = lax.broadcasted_iota(jnp.int32, s.shape, 1) + t * tile
            s = jnp.where(key_at <= query_at, s, -jnp.inf)
        top = jnp.max(s, axis=0, keepdims=True)
        if j < 2:
            top = jnp.where(visible[j], top, -jnp.inf)
        scores.append(s)
        tops.append(top)
    top = jnp.maximum(jnp.maximum(tops[0], tops[1]), tops[2])
    total = jnp.zeros_like(top)
    weights = []
    for j in range(3):
        shift = jnp.where(visible[j], top, jnp.inf) if j < 2 else top
        e = jnp.exp2(scores[j] - shift)
        total = total + jnp.sum(e, axis=0, keepdims=True)
        weights.append(e)
    inverse = 1.0 / total
    out_t = jnp.zeros((size, tile), F32)
    lows, probs = [], []
    for j in range(3):
        p = weights[j] * inverse
        low = p.astype(BF16)
        probs.append(p)
        lows.append(low)
        out_t = out_t + dot_nn(vt_ref[:, j * rows:j * rows + counts[j]], low)
    out_low = out_t.astype(BF16).astype(F32)
    row_dot = jnp.sum(do_t * out_low, axis=0, keepdims=True)
    dq_t = jnp.zeros((size, tile), F32)
    for j in range(3):
        dp = dot_nn(values[j, 0:counts[j], :], do_tb)
        ds = (probs[j] * (dp - row_dot)).astype(BF16)
        dq_t = dq_t + dot_nn(kt_ref[:, j * rows:j * rows + counts[j]], ds)
        dk_ref[j, 0:counts[j], :] += dot_nn(ds, q)
        dv_ref[j, 0:counts[j], :] += dot_nn(lows[j], do)
    return out_low.T.astype(BF16), (dq_t * scale).T.astype(BF16)


def step_kernel(blocks, halves, tile, sel_ref, kv_ref, own_ref, q_ref, do_ref, grads_ref, oo_ref, dqo_ref,
                qv, dov, near, send, ks, vs, kt, vt, dk, dv, down, outv, dqv, dnear, arrived, home, ret,
                s1, r1, s2, r2, xs, xr, xl, b1, c1, b2, c2, ys, yr, yl, *held):
    me, half = lax.axis_index("ctx"), lax.axis_index("head")
    heads, group, rows, size = qv.shape
    part = group // halves
    piece = kv_ref.shape[2]
    scale = size ** -0.5
    visible = [sel_ref[me, j] < me for j in range(2)]
    here = {"ctx": me, "head": half}
    greet(blocks, halves)

    def send_all(make):
        @pl.loop(1, blocks)
        def _(i):
            make(lax.rem(me + i, blocks)).start()

    def spread(n):
        send_all(lambda peer: pltpu.make_async_remote_copy(
            kv_ref.at[n, peer], held[n].at[me], s1.at[n], r1.at[n], device_id={"ctx": peer, "head": half}))

    spread(0)

    moves = []
    for e, (src, dst) in enumerate(((q_ref, qv), (do_ref, dov))):
        place = dst.at[:, pl.ds(half * part, part)]
        for i in range(1, halves):
            other = lax.rem(half + i, halves)
            moves.append(pltpu.make_async_remote_copy(
                src.at[pl.ds(other * heads, heads)], place, xs.at[e, i - 1], xr.at[e, i - 1],
                device_id={"ctx": me, "head": other}))
        moves.append(pltpu.make_async_copy(src.at[pl.ds(half * heads, heads)], place, xl.at[e]))
    for move in moves:
        move.start()

    def fetch_first(n):
        return pltpu.make_async_remote_copy(
            kv_ref.at[n, pl.ds(0, blocks - 1)], held[n].at[pl.ds(0, blocks - 1)], s1.at[n], r1.at[n],
            device_id=here)

    def fetch_last(n):
        return pltpu.make_async_remote_copy(
            send.at[n, pl.ds(0, blocks - 1)], near.at[n, :, pl.ds(0, blocks - 1)], s2.at[n], r2.at[n],
            device_id=here)

    def relay(n):
        held[n][me] = kv_ref[n, me]
        fetch_first(n).wait_recv()

        @pl.loop(0, blocks)
        def _(dest):
            for j in range(2):
                send[n, dest, j] = held[n][sel_ref[dest, j]]

        send_all(lambda dest: pltpu.make_async_remote_copy(
            send.at[n, dest], near.at[n, :, me], s2.at[n], r2.at[n], device_id={"ctx": dest, "head": half}))
        if n + 1 < heads:
            spread(n + 1)
        for j in range(2):
            near[n, j, me] = held[n][sel_ref[me, j]]

    relay(0)

    for move in moves:
        move.wait()

    def back_first(n):
        return pltpu.make_async_remote_copy(
            dnear.at[n, :, pl.ds(0, blocks - 1)], arrived.at[n, pl.ds(0, blocks - 1)], b1.at[n], c1.at[n],
            device_id=here)

    def back_last(n):
        return pltpu.make_async_remote_copy(
            home.at[n, pl.ds(0, blocks - 1)], ret.at[n, pl.ds(0, blocks - 1)], b2.at[n], c2.at[n],
            device_id=here)

    together = math.gcd(4, blocks)

    def collect(n):
        back_first(n).wait_recv()

        @pl.loop(0, blocks)
        def _(s):
            def add(c, total):
                for i in range(together):
                    b = c * together + i
                    for j in range(2):
                        mine = ((sel_ref[b, j] == s) & (b > s)).astype(F32)
                        total = total + arrived[n, b, j].astype(F32) * mine
                return total

            total = lax.fori_loop((s + 1) // together, blocks // together, add, jnp.zeros((piece, size), F32))
            home[n, s] = total.astype(BF16)

        send_all(lambda dest: pltpu.make_async_remote_copy(
            home.at[n, dest], ret.at[n, me], b2.at[n], c2.at[n], device_id={"ctx": dest, "head": half}))
        ret[n, me] = home[n, me]

    def results(n):
        made = []
        for e, (src, dst) in enumerate(((outv, oo_ref), (dqv, dqo_ref))):
            place = dst.at[half * heads + n]
            for i in range(1, halves):
                other = lax.rem(half + i, halves)
                made.append(pltpu.make_async_remote_copy(
                    src.at[n, pl.ds(other * part, part)], place, ys.at[n, e, i - 1], yr.at[n, e, i - 1],
                    device_id={"ctx": me, "head": other}))
            made.append(pltpu.make_async_copy(src.at[n, pl.ds(half * part, part)], place, yl.at[n, e]))
        return made

    def join(x):
        if piece % 16 == 0:
            return x.reshape(rows, size)
        return x.astype(F32).reshape(rows, size).astype(BF16)

    pieces = blocks // 2

    @pl.loop(0, heads * group)
    def _(at):
        n = at // group
        g = at % group

        @pl.when(g == 0)
        def _():
            fetch_last(n).wait_recv()
            for j in range(3):
                if j < 2:
                    k, v = join(near[n, j, 0:pieces]), join(near[n, j, pieces:2 * pieces])
                else:
                    k, v = own_ref[n, 0], own_ref[n, 1]
                ks[j] = k
                vs[j] = v
                kt[:, j * rows:(j + 1) * rows] = k.astype(F32).T.astype(BF16)
                vt[:, j * rows:(j + 1) * rows] = v.astype(F32).T.astype(BF16)
            dk[...] = jnp.zeros_like(dk)
            dv[...] = jnp.zeros_like(dv)

        for t in range(rows // tile):
            span = slice(t * tile, (t + 1) * tile)
            out, dq = attend_tile(t, tile, scale, visible, qv[n, g, span, :], dov[n, g, span, :],
                                  ks, vs, kt, vt, dk, dv)
            outv[n, g, span, :] = out
            dqv[n, g, span, :] = dq

        for m in range(1, heads):
            @pl.when(at == (m - 1) * group)
            def _(m=m):
                relay(m)

        @pl.when(g == group - 1)
        def _():
            for j in range(2):
                dnear[n, j, 0:pieces] = (dk[j] * scale).reshape(pieces, piece, size).astype(BF16)
                dnear[n, j, pieces:2 * pieces] = dv[j].reshape(pieces, piece, size).astype(BF16)
            down[n, 0:pieces] = (dk[2] * scale).reshape(pieces, piece, size)
            down[n, pieces:2 * pieces] = dv[2].reshape(pieces, piece, size)
            send_all(lambda peer: pltpu.make_async_remote_copy(
                dnear.at[n, :, peer], arrived.at[n, me], b1.at[n], c1.at[n],
                device_id={"ctx": peer, "head": half}))
            for j in range(2):
                arrived[n, me, j] = dnear[n, j, me]
            for move in results(n):
                move.start()

        @pl.when((n > 0) & (g == group - 2))
        def _():
            collect(n - 1)

    collect(heads - 1)
    for n in range(heads):
        fetch_first(n).wait_send()
        fetch_last(n).wait_send()
        back_first(n).wait_send()
        for move in results(n):
            move.wait()
    for n in range(heads):
        back_last(n).wait_send()
        back_last(n).wait_recv()
        grads_ref[n] = (ret[n].astype(F32) + down[n]).astype(BF16)


def step(selected, kv, own, q, do, blocks, halves):
    heads, _, piece, size = kv.shape
    full, part, rows, _ = q.shape
    group = part * halves
    tile = min(256, rows)
    near = pl.BlockSpec(memory_space=pltpu.VMEM)
    far = pl.BlockSpec(memory_space=pl.ANY)
    dma = pltpu.SemaphoreType.DMA
    vmem = pltpu.VMEM
    return pl.pallas_call(
        functools.partial(step_kernel, blocks, halves, tile),
        in_specs=[pl.BlockSpec(memory_space=pltpu.SMEM), near, near, far, far],
        out_specs=[near, far, far],
        out_shape=[jax.ShapeDtypeStruct(kv.shape, BF16), jax.ShapeDtypeStruct(q.shape, BF16),
                   jax.ShapeDtypeStruct(q.shape, BF16)],
        scratch_shapes=[
            vmem((heads, group, rows, size), BF16),
            vmem((heads, group, rows, size), BF16),
            vmem((heads, 2, blocks, piece, size), BF16),
            vmem((heads, blocks, 2, piece, size), BF16),
            vmem((3, rows, size), BF16),
            vmem((3, rows, size), BF16),
            vmem((size, 3 * rows), BF16),
            vmem((size, 3 * rows), BF16),
            vmem((3, rows, size), F32),
            vmem((3, rows, size), F32),
            vmem((heads, blocks, piece, size), F32),
            vmem((heads, group, rows, size), BF16),
            vmem((heads, group, rows, size), BF16),
            vmem((heads, 2, blocks, piece, size), BF16),
            vmem((heads, blocks, 2, piece, size), BF16),
            vmem((heads, blocks, piece, size), BF16),
            vmem((heads, blocks, piece, size), BF16),
            dma((heads,)), dma((heads,)), dma((heads,)), dma((heads,)),
            dma((2, halves - 1)), dma((2, halves - 1)), dma((2,)),
            dma((heads,)), dma((heads,)), dma((heads,)), dma((heads,)),
            dma((heads, 2, halves - 1)), dma((heads, 2, halves - 1)), dma((heads, 2)),
        ] + [vmem((blocks, piece, size), BF16)] * heads,
        compiler_params=pltpu.CompilerParams(collective_id=0, has_side_effects=True,
                                             vmem_limit_bytes=56 * 2**20),
    )(selected, kv, own, q, do)


def on_device(queries, keys, values, output_gradient, selected):
    rows, kv_count, size = keys.shape
    blocks, halves = lax.axis_size("ctx"), lax.axis_size("head")
    own_heads = kv_count // halves
    half = lax.axis_index("head")
    piece = 2 * rows // blocks
    own = jnp.stack([keys, values])
    own = lax.dynamic_slice_in_dim(own, half * own_heads, own_heads, 2)
    own = jnp.transpose(own, (2, 0, 1, 3))
    q, do = jnp.transpose(queries, (2, 1, 0, 3)), jnp.transpose(output_gradient, (2, 1, 0, 3))
    grads, out, dq = step(selected, own.reshape(own_heads, blocks, piece, size), own, q, do, blocks, halves)
    grads = jnp.transpose(grads.reshape(own.shape), (1, 2, 0, 3))
    return jnp.transpose(out, (2, 1, 0, 3)), jnp.transpose(dq, (2, 1, 0, 3)), grads[0], grads[1]


def solution(mesh):
    return jax.shard_map(
        on_device,
        mesh=mesh,
        in_specs=(
            P("ctx", "head", None, None),
            P("ctx", None, None),
            P("ctx", None, None),
            P("ctx", "head", None, None),
            P(),
        ),
        out_specs=(
            P("ctx", "head", None, None),
            P("ctx", "head", None, None),
            P("ctx", "head", None),
            P("ctx", "head", None),
        ),
        check_vma=False,
    )
```

```python
import functools
import math

import jax
import jax.numpy as jnp
from jax import lax
from jax.experimental import pallas as pl
from jax.experimental.pallas import tpu as pltpu
from jax.sharding import PartitionSpec as P

F32 = jnp.float32
BF16 = jnp.bfloat16


def dot_nt(a, b):
    return lax.dot_general(a, b, (((1,), (1,)), ((), ())), preferred_element_type=F32)


def dot_nn(a, b):
    return lax.dot_general(a, b, (((1,), (0,)), ((), ())), preferred_element_type=F32)


def greet(blocks, halves):
    me, half = lax.axis_index("ctx"), lax.axis_index("head")
    barrier = pltpu.get_barrier_semaphore()

    @pl.loop(1, blocks)
    def _(i):
        pl.semaphore_signal(barrier, inc=1, device_id={"ctx": lax.rem(me + i, blocks), "head": half})

    for i in range(1, halves):
        pl.semaphore_signal(barrier, inc=1, device_id={"ctx": me, "head": lax.rem(half + i, halves)})
    pl.semaphore_wait(barrier, blocks - 1 + halves - 1)


def attend_tile(t, tile, scale, visible, q, do, keys, values, kt_ref, vt_ref, dk_ref, dv_ref):
    rows, size = keys.shape[1], keys.shape[2]
    factor = scale * math.log2(math.e)
    do_t = do.astype(F32).T
    do_tb = do_t.astype(BF16)
    q_tb = q.astype(F32).T.astype(BF16)
    counts = (rows, rows, (t + 1) * tile)
    scores, tops = [], []
    for j in range(3):
        s = dot_nn(keys[j, 0:counts[j], :], q_tb) * factor
        if j == 2:
            key_at = lax.broadcasted_iota(jnp.int32, s.shape, 0)
            query_at = lax.broadcasted_iota(jnp.int32, s.shape, 1) + t * tile
            s = jnp.where(key_at <= query_at, s, -jnp.inf)
        top = jnp.max(s, axis=0, keepdims=True)
        if j < 2:
            top = jnp.where(visible[j], top, -jnp.inf)
        scores.append(s)
        tops.append(top)
    top = jnp.maximum(jnp.maximum(tops[0], tops[1]), tops[2])
    total = jnp.zeros_like(top)
    weights = []
    for j in range(3):
        shift = jnp.where(visible[j], top, jnp.inf) if j < 2 else top
        e = jnp.exp2(scores[j] - shift)
        total = total + jnp.sum(e, axis=0, keepdims=True)
        weights.append(e)
    inverse = 1.0 / total
    out_t = jnp.zeros((size, tile), F32)
    lows, probs = [], []
    for j in range(3):
        p = weights[j] * inverse
        low = p.astype(BF16)
        probs.append(p)
        lows.append(low)
        out_t = out_t + dot_nn(vt_ref[:, j * rows:j * rows + counts[j]], low)
    out_low = out_t.astype(BF16).astype(F32)
    row_dot = jnp.sum(do_t * out_low, axis=0, keepdims=True)
    dq_t = jnp.zeros((size, tile), F32)
    for j in range(3):
        dp = dot_nn(values[j, 0:counts[j], :], do_tb)
        ds = (probs[j] * (dp - row_dot)).astype(BF16)
        dq_t = dq_t + dot_nn(kt_ref[:, j * rows:j * rows + counts[j]], ds)
        dk_ref[j, 0:counts[j], :] += dot_nn(ds, q)
        dv_ref[j, 0:counts[j], :] += dot_nn(lows[j], do)
    return out_low.T.astype(BF16), (dq_t * scale).T.astype(BF16)


def step_kernel(blocks, halves, tile, sel_ref, kv_ref, own_ref, q_ref, do_ref, grads_ref, oo_ref, dqo_ref,
                qv, dov, near, send, ks, vs, kt, vt, dk, dv, down, outv, dqv, dnear, arrived, home, ret,
                s1, r1, s2, r2, xs, xr, xl, b1, c1, b2, c2, ys, yr, yl, *held):
    me, half = lax.axis_index("ctx"), lax.axis_index("head")
    heads, group, rows, size = qv.shape
    part = group // halves
    piece = kv_ref.shape[2]
    scale = size ** -0.5
    visible = [sel_ref[me, j] < me for j in range(2)]
    here = {"ctx": me, "head": half}
    greet(blocks, halves)

    def send_all(make):
        @pl.loop(1, blocks)
        def _(i):
            make(lax.rem(me + i, blocks)).start()

    def spread(n):
        send_all(lambda peer: pltpu.make_async_remote_copy(
            kv_ref.at[n, peer], held[n].at[me], s1.at[n], r1.at[n], device_id={"ctx": peer, "head": half}))

    spread(0)

    moves = []
    for e, (src, dst) in enumerate(((q_ref, qv), (do_ref, dov))):
        place = dst.at[:, pl.ds(half * part, part)]
        for i in range(1, halves):
            other = lax.rem(half + i, halves)
            moves.append(pltpu.make_async_remote_copy(
                src.at[pl.ds(other * heads, heads)], place, xs.at[e, i - 1], xr.at[e, i - 1],
                device_id={"ctx": me, "head": other}))
        moves.append(pltpu.make_async_copy(src.at[pl.ds(half * heads, heads)], place, xl.at[e]))
    for move in moves:
        move.start()

    def fetch_first(n):
        return pltpu.make_async_remote_copy(
            kv_ref.at[n, pl.ds(0, blocks - 1)], held[n].at[pl.ds(0, blocks - 1)], s1.at[n], r1.at[n],
            device_id=here)

    def fetch_last(n):
        return pltpu.make_async_remote_copy(
            send.at[n, pl.ds(0, blocks - 1)], near.at[n, :, pl.ds(0, blocks - 1)], s2.at[n], r2.at[n],
            device_id=here)

    def relay(n):
        held[n][me] = kv_ref[n, me]
        fetch_first(n).wait_recv()

        @pl.loop(0, blocks)
        def _(dest):
            for j in range(2):
                send[n, dest, j] = held[n][sel_ref[dest, j]]

        send_all(lambda dest: pltpu.make_async_remote_copy(
            send.at[n, dest], near.at[n, :, me], s2.at[n], r2.at[n], device_id={"ctx": dest, "head": half}))
        if n + 1 < heads:
            spread(n + 1)
        for j in range(2):
            near[n, j, me] = held[n][sel_ref[me, j]]

    relay(0)

    for move in moves:
        move.wait()

    def back_first(n):
        return pltpu.make_async_remote_copy(
            dnear.at[n, :, pl.ds(0, blocks - 1)], arrived.at[n, pl.ds(0, blocks - 1)], b1.at[n], c1.at[n],
            device_id=here)

    def back_last(n):
        return pltpu.make_async_remote_copy(
            home.at[n, pl.ds(0, blocks - 1)], ret.at[n, pl.ds(0, blocks - 1)], b2.at[n], c2.at[n],
            device_id=here)

    together = math.gcd(4, blocks)

    def collect(n):
        back_first(n).wait_recv()

        def deliver(i):
            dest = lax.rem(me + i, blocks)
            pltpu.make_async_remote_copy(
                home.at[n, dest], ret.at[n, me], b2.at[n], c2.at[n],
                device_id={"ctx": dest, "head": half}).start()

        @pl.loop(1, blocks + 1)
        def _(i):
            s = lax.rem(me + i, blocks)

            def add(c, total):
                for k in range(together):
                    b = c * together + k
                    for j in range(2):
                        mine = ((sel_ref[b, j] == s) & (b > s)).astype(F32)
                        total = total + arrived[n, b, j].astype(F32) * mine
                return total

            total = lax.fori_loop((s + 1) // together, blocks // together, add, jnp.zeros((piece, size), F32))
            home[n, s] = total.astype(BF16)

            @pl.when(i > 1)
            def _():
                deliver(i - 1)

        ret[n, me] = home[n, me]

    def results(n):
        made = []
        for e, (src, dst) in enumerate(((outv, oo_ref), (dqv, dqo_ref))):
            place = dst.at[half * heads + n]
            for i in range(1, halves):
                other = lax.rem(half + i, halves)
                made.append(pltpu.make_async_remote_copy(
                    src.at[n, pl.ds(other * part, part)], place, ys.at[n, e, i - 1], yr.at[n, e, i - 1],
                    device_id={"ctx": me, "head": other}))
            made.append(pltpu.make_async_copy(src.at[n, pl.ds(half * part, part)], place, yl.at[n, e]))
        return made

    def join(x):
        if piece % 16 == 0:
            return x.reshape(rows, size)
        return x.astype(F32).reshape(rows, size).astype(BF16)

    pieces = blocks // 2

    @pl.loop(0, heads * group)
    def _(at):
        n = at // group
        g = at % group

        @pl.when(g == 0)
        def _():
            fetch_last(n).wait_recv()
            for j in range(3):
                if j < 2:
                    k, v = join(near[n, j, 0:pieces]), join(near[n, j, pieces:2 * pieces])
                else:
                    k, v = own_ref[n, 0], own_ref[n, 1]
                ks[j] = k
                vs[j] = v
                kt[:, j * rows:(j + 1) * rows] = k.astype(F32).T.astype(BF16)
                vt[:, j * rows:(j + 1) * rows] = v.astype(F32).T.astype(BF16)
            dk[...] = jnp.zeros_like(dk)
            dv[...] = jnp.zeros_like(dv)

        for t in range(rows // tile):
            span = slice(t * tile, (t + 1) * tile)
            out, dq = attend_tile(t, tile, scale, visible, qv[n, g, span, :], dov[n, g, span, :],
                                  ks, vs, kt, vt, dk, dv)
            outv[n, g, span, :] = out
            dqv[n, g, span, :] = dq

        for m in range(1, heads):
            @pl.when(at == (m - 1) * group)
            def _(m=m):
                relay(m)

        @pl.when(g == group - 1)
        def _():
            for j in range(2):
                dnear[n, j, 0:pieces] = (dk[j] * scale).reshape(pieces, piece, size).astype(BF16)
                dnear[n, j, pieces:2 * pieces] = dv[j].reshape(pieces, piece, size).astype(BF16)
            down[n, 0:pieces] = (dk[2] * scale).reshape(pieces, piece, size)
            down[n, pieces:2 * pieces] = dv[2].reshape(pieces, piece, size)
            send_all(lambda peer: pltpu.make_async_remote_copy(
                dnear.at[n, :, peer], arrived.at[n, me], b1.at[n], c1.at[n],
                device_id={"ctx": peer, "head": half}))
            for j in range(2):
                arrived[n, me, j] = dnear[n, j, me]
            for move in results(n):
                move.start()

        @pl.when((n > 0) & (g == group - 2))
        def _():
            collect(n - 1)

    collect(heads - 1)
    for n in range(heads):
        fetch_first(n).wait_send()
        fetch_last(n).wait_send()
        back_first(n).wait_send()
        for move in results(n):
            move.wait()
    for n in range(heads):
        back_last(n).wait_send()
        back_last(n).wait_recv()
        grads_ref[n] = (ret[n].astype(F32) + down[n]).astype(BF16)


def step(selected, kv, own, q, do, blocks, halves):
    heads, _, piece, size = kv.shape
    full, part, rows, _ = q.shape
    group = part * halves
    tile = min(256, rows)
    near = pl.BlockSpec(memory_space=pltpu.VMEM)
    far = pl.BlockSpec(memory_space=pl.ANY)
    dma = pltpu.SemaphoreType.DMA
    vmem = pltpu.VMEM
    return pl.pallas_call(
        functools.partial(step_kernel, blocks, halves, tile),
        in_specs=[pl.BlockSpec(memory_space=pltpu.SMEM), near, near, far, far],
        out_specs=[near, far, far],
        out_shape=[jax.ShapeDtypeStruct(kv.shape, BF16), jax.ShapeDtypeStruct(q.shape, BF16),
                   jax.ShapeDtypeStruct(q.shape, BF16)],
        scratch_shapes=[
            vmem((heads, group, rows, size), BF16),
            vmem((heads, group, rows, size), BF16),
            vmem((heads, 2, blocks, piece, size), BF16),
            vmem((heads, blocks, 2, piece, size), BF16),
            vmem((3, rows, size), BF16),
            vmem((3, rows, size), BF16),
            vmem((size, 3 * rows), BF16),
            vmem((size, 3 * rows), BF16),
            vmem((3, rows, size), F32),
            vmem((3, rows, size), F32),
            vmem((heads, blocks, piece, size), F32),
            vmem((heads, group, rows, size), BF16),
            vmem((heads, group, rows, size), BF16),
            vmem((heads, 2, blocks, piece, size), BF16),
            vmem((heads, blocks, 2, piece, size), BF16),
            vmem((heads, blocks, piece, size), BF16),
            vmem((heads, blocks, piece, size), BF16),
            dma((heads,)), dma((heads,)), dma((heads,)), dma((heads,)),
            dma((2, halves - 1)), dma((2, halves - 1)), dma((2,)),
            dma((heads,)), dma((heads,)), dma((heads,)), dma((heads,)),
            dma((heads, 2, halves - 1)), dma((heads, 2, halves - 1)), dma((heads, 2)),
        ] + [vmem((blocks, piece, size), BF16)] * heads,
        compiler_params=pltpu.CompilerParams(collective_id=0, has_side_effects=True,
                                             vmem_limit_bytes=56 * 2**20),
    )(selected, kv, own, q, do)


def on_device(queries, keys, values, output_gradient, selected):
    rows, kv_count, size = keys.shape
    blocks, halves = lax.axis_size("ctx"), lax.axis_size("head")
    own_heads = kv_count // halves
    half = lax.axis_index("head")
    piece = 2 * rows // blocks
    own = jnp.stack([keys, values])
    own = lax.dynamic_slice_in_dim(own, half * own_heads, own_heads, 2)
    own = jnp.transpose(own, (2, 0, 1, 3))
    q, do = jnp.transpose(queries, (2, 1, 0, 3)), jnp.transpose(output_gradient, (2, 1, 0, 3))
    grads, out, dq = step(selected, own.reshape(own_heads, blocks, piece, size), own, q, do, blocks, halves)
    grads = jnp.transpose(grads.reshape(own.shape), (1, 2, 0, 3))
    return jnp.transpose(out, (2, 1, 0, 3)), jnp.transpose(dq, (2, 1, 0, 3)), grads[0], grads[1]


def solution(mesh):
    return jax.shard_map(
        on_device,
        mesh=mesh,
        in_specs=(
            P("ctx", "head", None, None),
            P("ctx", None, None),
            P("ctx", None, None),
            P("ctx", "head", None, None),
            P(),
        ),
        out_specs=(
            P("ctx", "head", None, None),
            P("ctx", "head", None, None),
            P("ctx", "head", None),
            P("ctx", "head", None),
        ),
        check_vma=False,
    )
```
